32 devices in a mesh: row: 8 (over z, y), col: 4 (over x, core).
Axes of the slice: x: 2, y: 2, z: 4, core: 2. Of those that a mesh axis runs over, the one named last changes fastest.
Arguments:
- amplitudes: bfloat16 [16384, 1024], P('col', 'row'), may hold values from -6 to 6
- integrals: bfloat16 [256, 64, 8192], P('row', None, 'col'), may hold values from -0.125 to 0.125
- slot_tiles: int32 [256, 128], P('row', 'col'), may hold values from 0 to 63, as said below
- tile_count: int32 [256, 4], P('row', 'col'), may hold values from 1 to 32, as said below
- denominator: float32 [16384, 1024], P(('row', 'col')), may hold values from 1 to 4
Outputs:
- update: bfloat16 [16384, 1024], P(('row', 'col'))
The draws below stay inside these ranges and needn't reach their ends.
Inputs may be any that keep to these rules, and one draw needn't show every extreme that they name: `slot_tiles`: within one residual tile and one column block, the 32 slots name distinct tiles. `tile_count`: in every column block some residual tile has all 32 slots live.
All inputs are finite; a program needn't handle non-finite values.
Results may differ from the reference program's by a relative error of at most 0.014.
Values may be sent and summed in bfloat16 or wider, within the bound.
A program may use at most 192 MiB of HBM per device.

```python
import math
import jax
import jax.numpy as jnp
from jax import lax

TILE = 64
K_DEV = 32
PAIRS = 1024
NT = 256
N_COL = 4


def draw_slot_tiles(key, part):
    block_tiles = NT // N_COL
    row_keys = jax.random.split(jax.random.fold_in(key, 11), NT * N_COL)
    picks = jax.vmap(lambda one_key: jax.random.permutation(one_key, block_tiles)[:K_DEV])(row_keys)
    return picks.reshape(NT, N_COL * K_DEV).astype(jnp.int32)


def draw_tile_count(key, part):
    counts = jax.random.randint(jax.random.fold_in(key, 21), (NT, N_COL), 1, K_DEV + 1)
    full_rows = jax.random.randint(jax.random.fold_in(key, 22), (N_COL,), 0, NT)
    row_ids = jnp.arange(NT, dtype=jnp.int32)[:, None]
    return jnp.where(row_ids == full_rows[None, :], K_DEV, counts).astype(jnp.int32)


def spiked(drawn, own_key, source, target, parts, factor):
    def block_of(axis_at):
        return (jnp.arange(drawn.shape[axis_at]) // (drawn.shape[axis_at] // parts)).reshape((-1,) + (1,) * (drawn.ndim - 1 - axis_at))

    first = jax.random.permutation(own_key, parts)[block_of(target)]
    second = (block_of(target) + parts // 2) % parts
    return jnp.where((block_of(source) == first) | (block_of(source) == second), factor * drawn, drawn)


def shard_levels(rng, shape, cuts, least, top_value):
    factor_of, own = 1.0, jax.random.fold_in(rng, 6)
    for dim, blocks in cuts:
        steps = jnp.exp(jax.random.uniform(jax.random.fold_in(own, dim), (blocks,), jnp.float32, least / len(cuts), top_value / len(cuts)))
        factor_of = factor_of * jnp.repeat(steps, shape[dim] // blocks).reshape([-1 if axis == dim else 1 for axis in range(len(shape))])
    return factor_of


def noise(key, extent, spread, bound, cuts=(), kind=jnp.bfloat16):
    entries = spread * jax.random.normal(key, extent, jnp.float32)
    if cuts:
        entries = entries * shard_levels(key, extent, cuts, -0.22, 0.18)
    return jnp.clip(entries, -bound, bound).astype(kind)


def noise_with(stream_key, dims, spread, most, shards, heavy, held_as=jnp.bfloat16):
    entries = spread * jax.random.normal(stream_key, dims, jnp.float32)
    if shards:
        entries = entries * shard_levels(stream_key, dims, shards, -0.22, 0.18)
    return jnp.clip(spiked(entries, jax.random.fold_in(stream_key, 3), *heavy), -most, most).astype(held_as)


def setup_inputs(seed: int = 0) -> dict:
    key_list = jax.random.split(jax.random.key(seed), 6)
    amplitudes = noise(key_list[0], (NT * TILE, PAIRS), 1.0, 6.0, ((0, 4), (1, 8)))
    integrals = noise_with(key_list[1], (NT, TILE, N_COL * K_DEV * TILE), (N_COL * K_DEV * TILE // 2) ** -0.5, 0.125, ((0, 8), (2, 4)), (2, 0, 8, 2.0))
    slot_tiles = draw_slot_tiles(jax.random.fold_in(key_list[5], 71), 0)
    tile_count = draw_tile_count(jax.random.fold_in(key_list[5], 71), 0)
    denominator = jnp.clip(jnp.exp(math.log(4.0) - 1.3862944 * jax.random.uniform(key_list[4], (NT * TILE, PAIRS), jnp.float32) ** shard_levels(key_list[4], (NT * TILE, PAIRS), ((0, 32),), -0.2, 0.2)), 1.0, 4.0)
    return dict(amplitudes=amplitudes, integrals=integrals, slot_tiles=slot_tiles, tile_count=tile_count, denominator=denominator)


def reference(amplitudes, integrals, slot_tiles, tile_count, denominator):
    panels = amplitudes.reshape(NT, TILE, PAIRS)
    block_tiles = NT // N_COL

    def one_tile(packed):
        weights, slot_row, count_row = packed
        summed = jnp.zeros((TILE, PAIRS), jnp.float32)
        for block_index in range(N_COL):
            chosen_ids = (slot_row[block_index * K_DEV:(block_index + 1) * K_DEV] + block_index * block_tiles).astype(jnp.int32)
            chosen = panels[chosen_ids]
            live_mask = (jnp.arange(K_DEV, dtype=jnp.int32) < count_row[block_index]).astype(jnp.bfloat16)
            chosen = chosen * live_mask[:, None, None]
            weight_block = weights[:, block_index * K_DEV * TILE:(block_index + 1) * K_DEV * TILE]
            partial_sum = jnp.dot(weight_block, chosen.reshape(K_DEV * TILE, PAIRS), preferred_element_type=jnp.float32)
            rounded = lax.optimization_barrier(partial_sum.astype(jnp.bfloat16))
            summed = summed + rounded.astype(jnp.float32)
        return summed

    residual = lax.map(one_tile, (integrals, slot_tiles, tile_count)).reshape(NT * TILE, PAIRS)
    return (residual / denominator).astype(jnp.bfloat16)
```

```python
import functools

import jax
import jax.numpy as jnp
from jax import lax
from jax.experimental import pallas as pl
from jax.experimental.pallas import tpu as pltpu
from jax.sharding import PartitionSpec as P

LANES = 128
PIECES = 2


def line_order(size, at):
    return sorted(range(size), key=lambda k: (abs(k - at), -min(k, size - 1 - k)))


def kernel(
    dims, slots_ref, count_ref, amp_ref, ints_ref, den_ref, out_ref,
    panel, tiles, dense, partial, landed, den, slots_in, count_in, table, table_ref,
    load_sem, ints_sem, send_sem, recv_sem, part_send_sem, part_recv_sem,
):
    n_row, n_col, na, nb = dims
    tile_rows = ints_ref.shape[0]
    tile_size = ints_ref.shape[1]
    depth, pairs = amp_ref.shape
    groups = ints_ref.shape[2] // LANES
    quarter = partial.shape[1] // n_col
    row, col = lax.axis_index("row"), lax.axis_index("col")
    pos, side = row // nb, row % nb

    def device(a, b):
        return {"row": a * nb + b}

    up, down, across = device(pos + 1, side), device(pos - 1, side), device(pos, 1 - side)
    has_up, has_down = pos < na - 1, pos > 0

    barrier = pltpu.get_barrier_semaphore()

    @pl.when(has_up)
    def _():
        pl.semaphore_signal(barrier, inc=1, device_id=up)

    @pl.when(has_down)
    def _():
        pl.semaphore_signal(barrier, inc=1, device_id=down)

    pl.semaphore_signal(barrier, inc=1, device_id=across)
    for k in range(1, n_col):
        pl.semaphore_signal(barrier, inc=1, device_id={"col": lax.rem(col + k, n_col)})
    pl.semaphore_wait(barrier, n_col + has_up.astype(jnp.int32) + has_down.astype(jnp.int32))

    def order(t):
        value = jnp.int32(0)
        for k in range(na):
            for i, which in enumerate(line_order(na, k)):
                value = value + jnp.where((pos == k) & (t == i), which, 0)
        return value

    def mine(t):
        return order(t) * nb + side

    def other(t):
        return order(t) * nb + 1 - side

    def hop(source, j, h, way):
        to = (up, down, across)[way]
        return pltpu.make_async_remote_copy(
            source, panel.at[j, h], send_sem.at[j, h, way], recv_sem.at[j, h], device_id=to
        )

    def each_hop(t, own, h, act):
        a = order(t)
        goes_up, goes_down = has_up & (a <= pos), has_down & (a >= pos)
        if not own and h < PIECES // 2:
            return
        if not own:
            goes_up, goes_down = goes_up & (a == 0), goes_down & (a == na - 1)
        pl.when(goes_up)(lambda: act(0))
        pl.when(goes_down)(lambda: act(1))
        if own and h < PIECES // 2:
            act(2)
        elif own:
            pl.when((a == pos) | ((a > 0) & (a < na - 1)))(lambda: act(2))

    def piece(h):
        return pl.ds(h * (depth // PIECES), depth // PIECES)

    def pass_on(t, own, h):
        j = mine(t) if own else other(t)
        hop(panel.at[j, h], j, h, 2).wait_recv()
        each_hop(t, own, h, lambda way: hop(panel.at[j, h], j, h, way).start())

    for h in range(PIECES):
        each_hop(jnp.int32(0), True, h, lambda way: hop(amp_ref.at[piece(h)], row, h, way).start())

    load_own = [
        pltpu.make_async_copy(amp_ref.at[piece(h)], panel.at[row, h], load_sem.at[1 + h]) for h in range(PIECES)
    ]
    load_den = pltpu.make_async_copy(den_ref, den, load_sem.at[0])
    load_small = [
        pltpu.make_async_copy(slots_ref, slots_in, load_sem.at[2 + PIECES]),
        pltpu.make_async_copy(count_ref, count_in, load_sem.at[3 + PIECES]),
    ]

    def load_ints(p):
        return pltpu.make_async_copy(
            ints_ref.at[:, :, pl.ds(p * LANES, LANES)],
            tiles.at[pl.ds(p * tile_rows, tile_rows)],
            ints_sem.at[p],
        )

    for copy in load_small:
        copy.start()
    for p in range(groups):
        load_ints(p).start()
    for copy in load_own:
        copy.start()
    load_den.start()
    for copy in load_small:
        copy.wait()

    virtual = lax.broadcasted_iota(jnp.int32, table.shape, 1)
    residual = lax.broadcasted_iota(jnp.int32, table.shape, 0)
    slots = slots_in[...]
    square = (tile_rows, tile_rows)
    diagonal = lax.broadcasted_iota(jnp.int32, square, 0) == lax.broadcasted_iota(jnp.int32, square, 1)
    count = jnp.sum(jnp.where(diagonal, count_in[...], 0), axis=1, keepdims=True)
    found = jnp.full(table.shape, 2 * groups * tile_rows, jnp.int32)
    for s in range(slots.shape[1]):
        turned = jnp.where(virtual % 2 != s % 2, groups * tile_rows, 0)
        hit = (slots[:, s:s + 1] == virtual) & (count > s)
        found = jnp.where(hit, turned + (s // 2 * tile_rows) + residual, found)
    table[...] = found

    batch = 8 if tile_rows % 8 == 0 else 1
    swapped = groups * tile_rows
    for p in range(groups):
        load_ints(p).wait()

        @pl.loop(0, tile_rows // batch)
        def _(a):
            x = tiles[pl.ds(p * tile_rows + a * batch, batch)]
            tiles[pl.ds(swapped + p * tile_rows + a * batch, batch)] = jnp.concatenate(
                [x[:, :, LANES // 2:], x[:, :, : LANES // 2]], axis=2
            )

    tiles[2 * swapped] = jnp.zeros((tile_size, LANES), jnp.bfloat16)
    load_table = pltpu.make_async_copy(table, table_ref, load_sem.at[1 + PIECES])
    load_table.start()
    load_table.wait()
    first = lax.broadcasted_iota(jnp.int32, (tile_size, LANES), 1) < LANES // 2

    @pl.loop(0, tile_rows)
    def _(a):
        for g in range(depth // LANES):
            dense[pl.ds(pl.multiple_of(a * tile_size, tile_size), tile_size), g * LANES:(g + 1) * LANES] = jnp.where(
                first, tiles[table_ref[a, 2 * g]], tiles[table_ref[a, 2 * g + 1]]
            )

    for copy in load_own:
        copy.wait()
    load_den.wait()

    def target(k):
        chip = lax.rem(col // 2 + k // 2, n_col // 2)
        return chip * 2 + lax.rem(col + k, 2)

    def rows_of(k):
        return pl.ds(pl.multiple_of(target(k) * quarter, quarter), quarter)

    def part_copy(j, k):
        return pltpu.make_async_remote_copy(
            partial.at[j, rows_of(k)], landed.at[k - 1, j],
            part_send_sem.at[j, k - 1], part_recv_sem.at[j, k - 1], device_id={"col": target(k)},
        )

    def multiply(*blocks):
        @pl.loop(0, n_col)
        def _(i):
            k = n_col - 1 - i
            rows = rows_of(k)
            right = [panel[j].reshape(depth, pairs) for j in blocks]
            right = right[0] if len(right) == 1 else jnp.concatenate(right, axis=1)
            product = jnp.dot(dense[rows, :], right, preferred_element_type=jnp.float32).astype(jnp.bfloat16)
            for n, j in enumerate(blocks):
                partial[j, rows, :] = product[:, n * pairs:(n + 1) * pairs]

            @pl.when(k > 0)
            def _():
                for j in blocks:
                    part_copy(j, k).start()

    def finish(*blocks):
        for j in blocks:
            for k in range(1, n_col):
                part_copy(j, k).wait_recv()
            total = partial[j, rows_of(0), :].astype(jnp.float32)
            for k in range(1, n_col):
                total = total + landed[k - 1, j].astype(jnp.float32)
            columns = pl.ds(pl.multiple_of(j * pairs, pairs), pairs)
            out_ref[:, columns] = (total / den[:, columns]).astype(jnp.bfloat16)

    def pass_block(t, own):
        for h in reversed(range(PIECES)) if not own else range(PIECES):
            pass_on(t, own, h)

    inside = has_up & has_down
    pass_block(jnp.int32(1), True)
    pl.when(inside)(lambda: pass_block(jnp.int32(2), True))
    pass_block(jnp.int32(0), False)
    multiply(row)

    @pl.loop(1, na)
    def _(t):
        @pl.when(t > 1)
        def _():
            pl.when(jnp.logical_not(inside))(lambda: pass_block(t, True))
            pass_block(t - 1, False)
            pl.when(inside & (t < na - 1))(lambda: pass_block(t + 1, True))

        multiply(mine(t), other(t - 1))

        @pl.when(t > 1)
        def _():
            finish(mine(t - 1), other(t - 2))

    last = jnp.int32(na - 1)
    pass_block(last, False)
    multiply(other(last))
    finish(row)
    finish(mine(last), other(last - 1))
    finish(other(last))

    @pl.loop(0, na)
    def _(t):
        for own in (True, False):
            j = mine(t) if own else other(t)
            for h in range(PIECES):
                each_hop(t, own, h, lambda way: hop(panel.at[j, h], j, h, way).wait_send())
            for k in range(1, n_col):
                part_copy(j, k).wait_send()


def fused(dims, amplitudes, integrals, slot_tiles, tile_count, denominator):
    n_row, n_col, na, nb = dims
    tile_rows, tile_size, width = integrals.shape
    depth, pairs = amplitudes.shape
    groups = width // LANES
    rows = tile_rows * tile_size
    dma = pltpu.SemaphoreType.DMA
    return pl.pallas_call(
        functools.partial(kernel, dims),
        out_shape=pltpu.VMEM(denominator.shape, jnp.bfloat16),
        in_specs=[pl.BlockSpec(memory_space=pl.ANY)] * 5,
        out_specs=pl.BlockSpec(memory_space=pltpu.VMEM),
        scratch_shapes=[
            pltpu.VMEM((n_row, PIECES, depth // PIECES, pairs), jnp.bfloat16),
            pltpu.VMEM((2 * groups * tile_rows + 1, tile_size, LANES), jnp.bfloat16),
            pltpu.VMEM((rows, depth), jnp.bfloat16),
            pltpu.VMEM((n_row, rows, pairs), jnp.bfloat16),
            pltpu.VMEM((n_col - 1, n_row, rows // n_col, pairs), jnp.bfloat16),
            pltpu.VMEM(denominator.shape, jnp.float32),
            pltpu.VMEM(slot_tiles.shape, jnp.int32),
            pltpu.VMEM((1, tile_rows), jnp.int32),
            pltpu.VMEM((tile_rows, -(-depth // tile_size // LANES) * LANES), jnp.int32),
            pltpu.SMEM((tile_rows, -(-depth // tile_size // LANES) * LANES), jnp.int32),
            dma((4 + PIECES,)),
            dma((groups,)),
            dma((n_row, PIECES, 3)),
            dma((n_row, PIECES)),
            dma((n_row, n_col - 1)),
            dma((n_row, n_col - 1)),
        ],
        compiler_params=pltpu.CompilerParams(
            collective_id=0, has_side_effects=True, vmem_limit_bytes=58 * 1024 * 1024
        ),
        name="ladder",
    )(slot_tiles, tile_count.reshape(1, -1), amplitudes, integrals, denominator)


def spread_weights(weights, slot_ids, live_count, block_tiles):
    tile_rows, tile_size, _ = weights.shape
    slot_total = slot_ids.shape[1]
    offsets = jnp.arange(slot_total, dtype=jnp.int32)
    live_mask = offsets[None, :] < live_count
    tile_ids = jnp.arange(block_tiles, dtype=jnp.int32)
    selector = ((slot_ids[:, :, None] == tile_ids[None, None, :]) & live_mask[:, :, None]).astype(
        jnp.bfloat16
    )
    shaped = weights.reshape(tile_rows, tile_size, slot_total, tile_size)
    spread = jnp.einsum(
        "nxsk,nsg->nxgk", shaped, selector, preferred_element_type=jnp.float32
    ).astype(jnp.bfloat16)
    return spread.reshape(tile_rows * tile_size, block_tiles * tile_size)


def plain(amplitudes, integrals, slot_tiles, tile_count, denominator):
    block_tiles = amplitudes.shape[0] // integrals.shape[1]
    dense = spread_weights(integrals, slot_tiles, tile_count, block_tiles)
    panel = lax.all_gather(amplitudes, "row", axis=1, tiled=True)
    residual = lax.psum_scatter(
        jnp.dot(dense, panel, preferred_element_type=jnp.float32).astype(jnp.bfloat16),
        "col",
        scatter_dimension=0,
        tiled=True,
    ).astype(jnp.float32)
    return (residual / denominator).astype(jnp.bfloat16)


def shards(n_row, n_col, amplitudes, *rest):
    nb = 2
    if amplitudes.shape[1] % LANES == 0 and n_row % nb == 0:
        return fused((n_row, n_col, n_row // nb, nb), amplitudes, *rest)
    return plain(amplitudes, *rest)


def solution(mesh):
    return jax.shard_map(
        functools.partial(shards, mesh.shape["row"], mesh.shape["col"]),
        mesh=mesh,
        in_specs=(
            P("col", "row"),
            P("row", None, "col"),
            P("row", "col"),
            P("row", "col"),
            P(("row", "col"), None),
        ),
        out_specs=P(("row", "col"), None),
        check_vma=False,
    )
```

```python
import functools

import jax
import jax.numpy as jnp
from jax import lax
from jax.experimental import pallas as pl
from jax.experimental.pallas import tpu as pltpu
from jax.sharding import PartitionSpec as P

LANES = 128
PIECES = 2
SHARES = (1, 1)


def cuts(depth):
    unit = depth // sum(SHARES)
    return [(sum(SHARES[:h]) * unit, SHARES[h] * unit) for h in range(PIECES)]


def line_order(size, at):
    return sorted(range(size), key=lambda k: (abs(k - at), -min(k, size - 1 - k)))


def kernel(
    dims, slots_ref, count_ref, amp_ref, ints_ref, den_ref, out_ref,
    panel, tiles, dense, partial, landed, den, slots_in, count_in, table, table_ref,
    load_sem, ints_sem, send_sem, recv_sem, part_send_sem, part_recv_sem, ready_sem,
):
    n_row, n_col, na, nb = dims
    tile_rows = ints_ref.shape[0]
    tile_size = ints_ref.shape[1]
    depth, pairs = amp_ref.shape
    groups = ints_ref.shape[2] // LANES
    quarter = partial.shape[1] // n_col
    row, col = lax.axis_index("row"), lax.axis_index("col")
    pos, side = row // nb, row % nb

    def device(a, b):
        return {"row": a * nb + b}

    up, down, across = device(pos + 1, side), device(pos - 1, side), device(pos, 1 - side)
    has_up, has_down = pos < na - 1, pos > 0

    barrier = pltpu.get_barrier_semaphore()

    @pl.when(has_up)
    def _():
        pl.semaphore_signal(barrier, inc=1, device_id=up)

    @pl.when(has_down)
    def _():
        pl.semaphore_signal(barrier, inc=1, device_id=down)

    pl.semaphore_signal(barrier, inc=1, device_id=across)
    for k in range(1, n_col):
        pl.when(col < k)(lambda: pl.semaphore_signal(barrier, inc=1, device_id={"col": k}))
    pl.semaphore_wait(barrier, 1 + col + has_up.astype(jnp.int32) + has_down.astype(jnp.int32))
    for k in range(n_col - 1):
        pl.when(col > k)(lambda: pl.semaphore_signal(ready_sem, inc=1, device_id={"col": k}))

    def order(t):
        value = jnp.int32(0)
        for k in range(na):
            for i, which in enumerate(line_order(na, k)):
                value = value + jnp.where((pos == k) & (t == i), which, 0)
        return value

    def mine(t):
        return order(t) * nb + side

    def other(t):
        return order(t) * nb + 1 - side

    parts = cuts(depth)
    inside = has_up & has_down

    def piece(h):
        return pl.ds(*parts[h])

    def hop(source, j, h, way):
        to = (up, down, across)[way]
        return pltpu.make_async_remote_copy(
            source.at[piece(h)], panel.at[j, piece(h)], send_sem.at[j, h, way], recv_sem.at[j, h], device_id=to
        )

    def each_hop(t, own, h, source, j, act):
        def go(way):
            act(hop(source, j, h, way))

        a = order(t)
        goes_up, goes_down = has_up & (a <= pos), has_down & (a >= pos)
        if not own and h < PIECES // 2:
            return
        if not own:
            goes_up, goes_down = goes_up & (a == 0), goes_down & (a == na - 1)
        pl.when(goes_up)(lambda: go(0))
        pl.when(goes_down)(lambda: go(1))
        if own and h < PIECES // 2:
            go(2)
        elif own:
            pl.when((a == pos) | ((a > 0) & (a < na - 1)))(lambda: go(2))

    def pass_on(t, own, h):
        j = mine(t) if own else other(t)
        hop(panel.at[j], j, h, 2).wait_recv()
        each_hop(t, own, h, panel.at[j], j, lambda copy: copy.start())

    for h in range(PIECES):
        each_hop(jnp.int32(0), True, h, amp_ref, row, lambda copy: copy.start())

    load_own = [
        pltpu.make_async_copy(amp_ref.at[piece(h)], panel.at[row, piece(h)], load_sem.at[1 + h]) for h in range(PIECES)
    ]
    load_den = pltpu.make_async_copy(den_ref, den, load_sem.at[0])
    load_small = [
        pltpu.make_async_copy(slots_ref, slots_in, load_sem.at[2 + PIECES]),
        pltpu.make_async_copy(count_ref, count_in, load_sem.at[3 + PIECES]),
    ]

    def load_ints(p):
        return pltpu.make_async_copy(
            ints_ref.at[:, :, pl.ds(p * LANES, LANES)],
            tiles.at[pl.ds(p * tile_rows, tile_rows)],
            ints_sem.at[p],
        )

    for copy in load_small:
        copy.start()
    for p in range(groups):
        load_ints(p).start()
    for copy in load_own:
        copy.start()
    load_den.start()
    for copy in load_small:
        copy.wait()

    virtual = lax.broadcasted_iota(jnp.int32, table.shape, 1)
    residual = lax.broadcasted_iota(jnp.int32, table.shape, 0)
    slots = slots_in[...]
    square = (tile_rows, tile_rows)
    diagonal = lax.broadcasted_iota(jnp.int32, square, 0) == lax.broadcasted_iota(jnp.int32, square, 1)
    count = jnp.sum(jnp.where(diagonal, count_in[...], 0), axis=1, keepdims=True)
    found = jnp.full(table.shape, 2 * groups * tile_rows, jnp.int32)
    for s in range(slots.shape[1]):
        turned = jnp.where(virtual % 2 != s % 2, groups * tile_rows, 0)
        hit = (slots[:, s:s + 1] == virtual) & (count > s)
        found = jnp.where(hit, turned + (s // 2 * tile_rows) + residual, found)
    table[...] = found

    batch = 8 if tile_rows % 8 == 0 else 1
    swapped = groups * tile_rows
    for p in range(groups):
        load_ints(p).wait()

        @pl.loop(0, tile_rows // batch)
        def _(a):
            x = tiles[pl.ds(p * tile_rows + a * batch, batch)]
            tiles[pl.ds(swapped + p * tile_rows + a * batch, batch)] = jnp.concatenate(
                [x[:, :, LANES // 2:], x[:, :, : LANES // 2]], axis=2
            )

    tiles[2 * swapped] = jnp.zeros((tile_size, LANES), jnp.bfloat16)
    load_table = pltpu.make_async_copy(table, table_ref, load_sem.at[1 + PIECES])
    load_table.start()
    load_table.wait()
    first = lax.broadcasted_iota(jnp.int32, (tile_size, LANES), 1) < LANES // 2

    @pl.loop(0, tile_rows)
    def _(a):
        for g in range(depth // LANES):
            dense[pl.ds(pl.multiple_of(a * tile_size, tile_size), tile_size), g * LANES:(g + 1) * LANES] = jnp.where(
                first, tiles[table_ref[a, 2 * g]], tiles[table_ref[a, 2 * g + 1]]
            )

    for copy in load_own:
        copy.wait()
    load_den.wait()

    chips, chip, core = n_col // 2, col // 2, lax.rem(col, 2)

    def target(i):
        return lax.rem(chip + i // 2 + 1, chips) * 2 + lax.rem(core + 1 + i, 2)

    def rows_of(i):
        return pl.ds(pl.multiple_of(target(i) * quarter, quarter), quarter)

    def part_copy(j, i):
        return pltpu.make_async_remote_copy(
            partial.at[j, rows_of(i)], landed.at[i, j],
            part_send_sem.at[j, i], part_recv_sem.at[j, i], device_id={"col": target(i)},
        )

    def hand_out(i, *blocks):
        @pl.when(i < n_col - 1)
        def _():
            for j in blocks:
                part_copy(j, i).start()

    def multiply(*blocks):
        @pl.loop(0, n_col)
        def _(i):
            rows = rows_of(i)
            right = [panel[j] for j in blocks]
            right = right[0] if len(right) == 1 else jnp.concatenate(right, axis=1)
            product = jnp.dot(dense[rows, :], right, preferred_element_type=jnp.float32).astype(jnp.bfloat16)
            for n, j in enumerate(blocks):
                partial[j, rows, :] = product[:, n * pairs:(n + 1) * pairs]
            hand_out(i, *blocks)

    def finish(j):
        total = partial[j, rows_of(n_col - 1), :].astype(jnp.float32)
        for i in range(n_col - 2, -1, -1):
            part_copy(j, i).wait_recv()
            total = total + landed[i, j].astype(jnp.float32)
        columns = pl.ds(pl.multiple_of(j * pairs, pairs), pairs)
        out_ref[:, columns] = (total / den[:, columns]).astype(jnp.bfloat16)

    def pass_block(t, own):
        for h in reversed(range(PIECES)) if not own else range(PIECES):
            pass_on(t, own, h)

    pass_block(jnp.int32(1), True)
    pl.when(inside)(lambda: pass_block(jnp.int32(2), True))
    pass_block(jnp.int32(0), False)
    pl.when(col < n_col - 1)(lambda: pl.semaphore_wait(ready_sem, n_col - 1 - col))
    multiply(row)

    @pl.loop(1, na)
    def _(t):
        @pl.when(t > 1)
        def _():
            pl.when(jnp.logical_not(inside))(lambda: pass_block(t, True))
            pass_block(t - 1, False)
            pl.when(inside & (t < na - 1))(lambda: pass_block(t + 1, True))

        multiply(mine(t), other(t - 1))

        @pl.when(t == 1)
        def _():
            finish(row)

        @pl.when((t > 1) & (t < na - 1))
        def _():
            finish(mine(t - 1))
            finish(other(t - 2))

    last = jnp.int32(na - 1)
    pass_block(last, False)
    multiply(other(last))
    def sent(j):
        for i in range(n_col - 1):
            part_copy(j, i).wait_send()

    @pl.loop(0, na)
    def _(t):
        for own in (True, False):
            j = mine(t) if own else other(t)
            for h in range(PIECES):
                each_hop(t, own, h, panel.at[j], j, lambda copy: copy.wait_send())
            if own:
                sent(j)
            else:
                pl.when(t < na - 1)(lambda: sent(j))

    if na > 2:
        finish(mine(last - 1))
        finish(other(last - 2))
    finish(mine(last))
    finish(other(last - 1))
    finish(other(last))
    sent(other(last))


def fused(dims, amplitudes, integrals, slot_tiles, tile_count, denominator):
    n_row, n_col, na, nb = dims
    tile_rows, tile_size, width = integrals.shape
    depth, pairs = amplitudes.shape
    groups = width // LANES
    rows = tile_rows * tile_size
    dma = pltpu.SemaphoreType.DMA
    return pl.pallas_call(
        functools.partial(kernel, dims),
        out_shape=pltpu.VMEM(denominator.shape, jnp.bfloat16),
        in_specs=[pl.BlockSpec(memory_space=pl.ANY)] * 5,
        out_specs=pl.BlockSpec(memory_space=pltpu.VMEM),
        scratch_shapes=[
            pltpu.VMEM((n_row, depth, pairs), jnp.bfloat16),
            pltpu.VMEM((2 * groups * tile_rows + 1, tile_size, LANES), jnp.bfloat16),
            pltpu.VMEM((rows, depth), jnp.bfloat16),
            pltpu.VMEM((n_row, rows, pairs), jnp.bfloat16),
            pltpu.VMEM((n_col - 1, n_row, rows // n_col, pairs), jnp.bfloat16),
            pltpu.VMEM(denominator.shape, jnp.float32),
            pltpu.VMEM(slot_tiles.shape, jnp.int32),
            pltpu.VMEM((1, tile_rows), jnp.int32),
            pltpu.VMEM((tile_rows, -(-depth // tile_size // LANES) * LANES), jnp.int32),
            pltpu.SMEM((tile_rows, -(-depth // tile_size // LANES) * LANES), jnp.int32),
            dma((4 + PIECES,)),
            dma((groups,)),
            dma((n_row, PIECES, 3)),
            dma((n_row, PIECES)),
            dma((n_row, n_col - 1)),
            dma((n_row, n_col - 1)),
            pltpu.SemaphoreType.REGULAR,
        ],
        compiler_params=pltpu.CompilerParams(
            collective_id=0, has_side_effects=True, vmem_limit_bytes=58 * 1024 * 1024
        ),
        name="ladder",
    )(slot_tiles, tile_count.reshape(1, -1), amplitudes, integrals, denominator)


def spread_weights(weights, slot_ids, live_count, block_tiles):
    tile_rows, tile_size, _ = weights.shape
    slot_total = slot_ids.shape[1]
    offsets = jnp.arange(slot_total, dtype=jnp.int32)
    live_mask = offsets[None, :] < live_count
    tile_ids = jnp.arange(block_tiles, dtype=jnp.int32)
    selector = ((slot_ids[:, :, None] == tile_ids[None, None, :]) & live_mask[:, :, None]).astype(
        jnp.bfloat16
    )
    shaped = weights.reshape(tile_rows, tile_size, slot_total, tile_size)
    spread = jnp.einsum(
        "nxsk,nsg->nxgk", shaped, selector, preferred_element_type=jnp.float32
    ).astype(jnp.bfloat16)
    return spread.reshape(tile_rows * tile_size, block_tiles * tile_size)


def plain(amplitudes, integrals, slot_tiles, tile_count, denominator):
    block_tiles = amplitudes.shape[0] // integrals.shape[1]
    dense = spread_weights(integrals, slot_tiles, tile_count, block_tiles)
    panel = lax.all_gather(amplitudes, "row", axis=1, tiled=True)
    residual = lax.psum_scatter(
        jnp.dot(dense, panel, preferred_element_type=jnp.float32).astype(jnp.bfloat16),
        "col",
        scatter_dimension=0,
        tiled=True,
    ).astype(jnp.float32)
    return (residual / denominator).astype(jnp.bfloat16)


def shards(n_row, n_col, amplitudes, *rest):
    nb = 2
    if amplitudes.shape[1] % LANES == 0 and n_row % nb == 0 and n_row > nb and n_col % 2 == 0 and amplitudes.shape[0] % (sum(SHARES) * LANES) == 0:
        return fused((n_row, n_col, n_row // nb, nb), amplitudes, *rest)
    return plain(amplitudes, *rest)


def solution(mesh):
    return jax.shard_map(
        functools.partial(shards, mesh.shape["row"], mesh.shape["col"]),
        mesh=mesh,
        in_specs=(
            P("col", "row"),
            P("row", None, "col"),
            P("row", "col"),
            P("row", "col"),
            P(("row", "col"), None),
        ),
        out_specs=P(("row", "col"), None),
        check_vma=False,
    )
```
